512 devices in a mesh: seq: 8 (over z), vocab: 64 (over y, x, core).
Axes of the slice: x: 4, y: 8, z: 8, core: 2. Of those that a mesh axis runs over, the one named last changes fastest.
Arguments:
- hidden: bfloat16 [2048, 8192], P('seq', 'vocab'), may hold values from -120 to 120
- head_weight: bfloat16 [8192, 98304], P('seq', 'vocab'), may hold values from -0.0625 to 0.0625
- vocab_basis: bfloat16 [98304, 1024], P('vocab', 'seq'), may hold values from -0.0048828125 to 0.0048828125
- keep_index: int32 [512], P('seq'), may hold values from 0 to 255, as said below
- counts: int32 [8], P('seq'), may hold values from 1 to 64, as said below
Outputs:
- coefficients: float32 [512, 1024], P('seq', 'vocab')
The draws below stay inside these ranges and needn't reach their ends.
Inputs may be any that keep to these rules, and one draw needn't show every extreme that they name: `keep_index`: each owner's list is strictly increasing and ends at 255. `counts`: exactly one owner has all 64 slots live.
All inputs are finite; a program needn't handle non-finite values.
Results may differ from the reference program's by a relative error of at most 0.0032.
Values may be sent and summed in bfloat16 or wider, within the bound.
No kernel may reach another device: no remote copies, remote signals or barrier semaphores. Data moves between devices by JAX's collectives and lax.ppermute only.
A program may use at most 64 MiB of HBM per device.

```python
import math
import jax
import jax.numpy as jnp

D = 8192
V = 98304
R = 1024
CAP = 64
POS = 256
N_SEQ = 8


def draw_hidden(key, part):
    subkeys = jax.random.split(key, 2)
    values = jax.random.truncated_normal(subkeys[0], -6.0, 6.0, (N_SEQ * POS, D), jnp.float32)
    scales = 2.0 * jnp.exp(jax.random.uniform(subkeys[1], (N_SEQ * POS, 1), jnp.float32, 0.0, math.log(10.0)))
    return (values * scales).astype(jnp.bfloat16)


def owner_list(owner_key):
    chosen = jax.random.permutation(owner_key, POS - 1)[:CAP - 1]
    joined = jnp.concatenate([chosen.astype(jnp.int32), jnp.full((1,), POS - 1, jnp.int32)])
    return jnp.sort(joined)


def draw_keep_index(key, part):
    owner_keys = jax.random.split(jax.random.fold_in(key, 11), N_SEQ)
    return jax.vmap(owner_list)(owner_keys).reshape(N_SEQ * CAP).astype(jnp.int32)


def draw_counts(key, part):
    subkeys = jax.random.split(jax.random.fold_in(key, 23), 2)
    values = jax.random.randint(subkeys[0], (N_SEQ,), 1, CAP)
    busiest = jax.random.randint(subkeys[1], (), 0, N_SEQ)
    return values.at[busiest].set(CAP).astype(jnp.int32)


def block_scale(stream_key, extent, shards, low, high):
    loudness, own = 1.0, jax.random.fold_in(stream_key, 6)
    for axis_at, shards_of in shards:
        heights = jnp.exp(jax.random.uniform(jax.random.fold_in(own, axis_at), (shards_of,), jnp.float32, low / len(shards), high / len(shards)))
        loudness = loudness * jnp.repeat(heights, extent[axis_at] // shards_of).reshape([-1 if axis == axis_at else 1 for axis in range(len(extent))])
    return loudness


def gaussian(rng, dims, width, most, cuts=(), held_as=jnp.bfloat16):
    entries = jax.random.normal(rng, dims, jnp.float32) * width
    if len(cuts) > 0:
        entries = block_scale(rng, dims, cuts, -0.22, 0.18) * entries
    return jnp.clip(entries, min=-most, max=most).astype(held_as)


def setup_inputs(seed: int = 0) -> dict:
    seeds = jax.random.split(jax.random.key(seed), 6)
    return {
        "hidden": draw_hidden(jax.random.fold_in(seeds[5], 71), 0),
        "head_weight": gaussian(seeds[1], (D, V), D ** -0.5, 0.0625, ((0, 8), (1, 64))),
        "vocab_basis": gaussian(seeds[2], (V, R), (16 * V) ** -0.5, 0.0048828125, ((0, 64), (1, 8))),
        "keep_index": draw_keep_index(jax.random.fold_in(seeds[5], 71), 0),
        "counts": draw_counts(jax.random.fold_in(seeds[5], 71), 0),
    }


def reference(hidden, head_weight, vocab_basis, keep_index, counts):
    slot_ids = jnp.arange(N_SEQ * CAP, dtype=jnp.int32)
    owner_ids = slot_ids // CAP
    row_ids = (owner_ids * POS + keep_index).astype(jnp.int32)
    selected = hidden[row_ids]
    logits = jnp.dot(selected, head_weight, preferred_element_type=jnp.float32)
    row_max = jnp.max(logits, axis=1, keepdims=True)
    weights = jnp.exp(logits - row_max)
    denominator = jnp.sum(weights, axis=1, keepdims=True)
    expected = jnp.sum(weights * logits, axis=1, keepdims=True) / denominator
    centred = (logits - expected).astype(jnp.bfloat16)
    projected = jnp.dot(centred, vocab_basis, preferred_element_type=jnp.float32)
    live_rows = (slot_ids % CAP) < counts[owner_ids]
    return jnp.where(live_rows[:, None], projected, jnp.float32(0.0))
```

```python
import jax
import jax.numpy as jnp
from jax import lax
from jax.experimental import pallas as pl
from jax.experimental.pallas import tpu as pltpu
from jax.sharding import Mesh, PartitionSpec as P

F32 = jnp.float32
BF16 = jnp.bfloat16
Z = ("zh", "zl")
ALL = ("zh", "zl", "y", "x", "c")
VMEM = pl.BlockSpec(memory_space=pltpu.VMEM)
SMEM = pl.BlockSpec(memory_space=pltpu.SMEM)


def call(kernel, out_shape, in_specs, *args, scratch=()):
    multi = isinstance(out_shape, (list, tuple))
    return pl.pallas_call(
        kernel,
        out_shape=out_shape,
        in_specs=in_specs,
        out_specs=[VMEM] * len(out_shape) if multi else VMEM,
        scratch_shapes=list(scratch),
    )(*args)


def select_kernel(index_ref, hidden_ref, out_ref):
    rows = lax.broadcasted_iota(jnp.int32, (256, 64), 0)
    chosen = jnp.where(rows == index_ref[...], 1.0, 0.0).astype(BF16)
    picked = lax.dot_general(
        chosen, hidden_ref[...], (((0,), (0,)), ((), ())), preferred_element_type=F32
    ).astype(BF16)
    for i in range(8):
        out_ref[i] = picked


def logits_kernel(core_ref, own_ref, other_ref, head_ref, out_ref):
    first = core_ref[0] == 0
    for half in range(2):
        rows = pl.ds(half * 256, 256)
        features = []
        for x in range(4):
            own, other = own_ref[x, rows, :], other_ref[x, rows, :]
            features.append(jnp.where(first, own, other))
            features.append(jnp.where(first, other, own))
        lhs = jnp.concatenate(features, axis=1)
        for n in range(6):
            part = jnp.dot(
                lhs, head_ref[:, n * 256 : (n + 1) * 256], preferred_element_type=F32
            ).astype(BF16)
            for t in range(2):
                tile = 2 * n + t
                lanes = pl.ds((tile % 3) * 128, 128)
                out_ref[half * 4 + tile // 3, :, lanes] = part[:, t * 128 : (t + 1) * 128]


def project_kernel(core_ref, parts_ref, basis_ref, keep_ref, send_ref, cols_ref, extra_ref):
    core = core_ref[0]
    logits = parts_ref[0].astype(F32)
    for i in range(1, 8):
        logits = logits + parts_ref[i].astype(F32)
    top = jnp.max(logits, axis=1, keepdims=True)
    weights = jnp.exp(logits - top)
    denominator = jnp.sum(weights, axis=1, keepdims=True)
    weighted = jnp.sum(weights * logits, axis=1, keepdims=True)
    lane = lax.broadcasted_iota(jnp.int32, (256, 128), 1)
    stats = jnp.where(lane == 0, top, jnp.where(lane == 1, denominator, jnp.where(lane == 2, weighted, 0.0)))
    extra_ref[...] = stats.T[0:8, :]
    high = logits.astype(BF16)
    low = (logits - high.astype(F32)).astype(BF16)
    lhs = jnp.concatenate([high, low, jnp.ones((16, 384), BF16)], axis=0)
    for j in range(4):
        rhs = jnp.concatenate([basis_ref[2 * j], basis_ref[2 * j + 1]], axis=1)
        both = jnp.dot(lhs, rhs, preferred_element_type=F32)
        turned = (both[0:256] + both[256:512]).T
        extra_ref[4 + j : 5 + j, :] = both[512:513]
        for y in range(2):
            for x in range(4):
                for c in range(2):
                    start = y * 128 + x * 32 + c * 16
                    cols_ref[c, x, 2 * j + y] = turned[start : start + 16]
    keep_ref[0:512, :] = cols_ref[core].reshape(512, 256)
    send_ref[0:512, :] = cols_ref[1 - core].reshape(512, 256)
    keep_ref[512:520, :] = extra_ref[...]
    send_ref[512:520, :] = extra_ref[...]


def combine(extras):
    top = extras[0][0:1]
    for e in extras[1:]:
        top = jnp.maximum(top, e[0:1])
    row = lax.broadcasted_iota(jnp.int32, extras[0].shape, 0)
    total = None
    for e in extras:
        scaled = jnp.where(row < 3, e * jnp.exp(e[0:1] - top), e)
        total = scaled if total is None else total + scaled
    return jnp.where(row == 0, top, total)


def core_kernel(keep_ref, recv_ref, out_ref):
    extra = combine([keep_ref[512:520, :], recv_ref[512:520, :]])
    for x in range(4):
        rows = pl.ds(x * 128, 128)
        out_ref[x, 0:128, :] = keep_ref[rows, :] + recv_ref[rows, :]
        out_ref[x, 128:136, :] = extra


def x_kernel(in_ref, out_ref):
    extra = combine([in_ref[i, 128:136, :] for i in range(4)])
    for y in range(8):
        rows = pl.ds(y * 16, 16)
        out_ref[y, 0:16, :] = (in_ref[0, rows, :] + in_ref[1, rows, :]) + (in_ref[2, rows, :] + in_ref[3, rows, :])
        out_ref[y, 16:24, :] = extra


def y_kernel(place_ref, in_ref, out_ref):
    extra = combine([in_ref[i, 16:24, :] for i in range(8)])
    total = in_ref[0, 0:16, :]
    for i in range(1, 8):
        total = total + in_ref[i, 0:16, :]
    row = lax.broadcasted_iota(jnp.int32, (8, 256), 0)
    line = jnp.sum(jnp.where(row == 4 + place_ref[0], extra, 0.0), axis=0, keepdims=True)
    lane = lax.broadcasted_iota(jnp.int32, (16, 256), 1)
    sub = lax.broadcasted_iota(jnp.int32, (16, 256), 0)
    sums = jnp.sum(jnp.where(lane == sub + place_ref[1], line, 0.0), axis=1, keepdims=True)
    low = lax.broadcasted_iota(jnp.int32, (16, 128), 1) < 64
    for o in range(4):
        lanes = slice((o // 2) * 128, (o // 2) * 128 + 128)
        block, stats = total[:, lanes], extra[:, lanes]
        if o % 2:
            block, stats = pltpu.roll(block, 64, 1), pltpu.roll(stats, 64, 1)
        out_ref[o, 0:16, :] = jnp.where(low, block, sums)
        out_ref[o, 16:24, :] = stats


def finish_kernel(count_ref, in_ref, out_ref):
    total = in_ref[0, 0:16, :]
    for i in range(1, 4):
        total = total + in_ref[i, 0:16, :]
    stats = combine([in_ref[i, 16:24, :] for i in range(4)])
    expected = stats[2:3] / stats[1:2]
    result = total - expected * total[:, 64:65]
    lane = lax.broadcasted_iota(jnp.int32, (16, 128), 1)
    result = jnp.where(lane < count_ref[0], result, 0.0)
    out_ref[...] = result.T[0:64, :]


def shards(hidden, head_weight, vocab_basis, keep_index, counts):
    def shape(*dims, dtype=F32):
        return jax.ShapeDtypeStruct(dims, dtype)

    def exchange(v, axes):
        return lax.all_to_all(v, axes, 0, 0, tiled=True)

    def swap(v):
        return lax.ppermute(v, "c", [(0, 1), (1, 0)])

    core = lax.axis_index("c").astype(jnp.int32)
    column = lax.axis_index("y") * 128 + lax.axis_index("x") * 32 + core * 16
    place = jnp.stack([column // 256, column % 256]).astype(jnp.int32)
    core = core.reshape(1)

    owned = call(select_kernel, shape(8, 64, 128, dtype=BF16), [VMEM, VMEM], keep_index.reshape(1, 64), hidden)
    sliced = exchange(exchange(owned, "y"), Z)
    basis_parts = jnp.broadcast_to(vocab_basis.reshape(1, 4, 384, 128), (2, 4, 384, 128)).reshape(8, 384, 128)
    basis = exchange(basis_parts, Z)
    mine = exchange(jnp.broadcast_to(sliced.reshape(1, 512, 128), (4, 512, 128)), "x")
    theirs = swap(mine)
    parts = call(
        logits_kernel, shape(8, 256, 384, dtype=BF16), [SMEM, VMEM, VMEM, VMEM], core, mine, theirs, head_weight
    )
    parts = exchange(parts, Z)
    keep, send = call(
        project_kernel,
        [shape(520, 256), shape(520, 256)],
        [SMEM, VMEM, VMEM],
        core,
        parts,
        basis,
        scratch=[pltpu.VMEM((2, 4, 8, 16, 256), F32), pltpu.VMEM((8, 256), F32)],
    )
    sums = call(core_kernel, shape(4, 136, 256), [VMEM, VMEM], keep, swap(send))
    sums = call(x_kernel, shape(8, 24, 256), [VMEM], exchange(sums, "x"))
    sums = call(y_kernel, shape(4, 24, 128), [SMEM, VMEM], place, exchange(sums, "y"))
    return call(finish_kernel, shape(64, 16), [SMEM, VMEM], counts, exchange(sums, "zl"))


def solution(mesh):
    grid = Mesh(mesh.devices.reshape(2, 4, 8, 4, 2), ALL)
    rows, cols = ("zh", "zl"), ("y", "x", "c")
    in_specs = (P(rows, cols), P(rows, cols), P(cols, rows), P(rows), P(rows))
    return jax.shard_map(shards, mesh=grid, in_specs=in_specs, out_specs=P(rows, cols), check_vma=False)
```

```python
import jax
import jax.numpy as jnp
from jax import lax
from jax.experimental import pallas as pl
from jax.experimental.pallas import tpu as pltpu
from jax.sharding import Mesh, PartitionSpec as P


F32 = jnp.float32
BF16 = jnp.bfloat16
G = 4
LANES = 64 * G
PART = 1536 // G
Z = ("zh", "zl")
ALL = ("zh", "zl", "y", "x", "c")
VMEM = pl.BlockSpec(memory_space=pltpu.VMEM)
SMEM = pl.BlockSpec(memory_space=pltpu.SMEM)
OUTER = pl.BlockSpec(memory_space=pltpu.VMEM)
STAY = pl.BlockSpec(memory_space=pl.ANY)


def call(kernel, out_shape, in_specs, *args, scratch=(), out_memory=pltpu.VMEM):
    args = [
        pltpu.with_memory_space_constraint(a, pltpu.VMEM) if spec is VMEM else a
        for a, spec in zip(args, in_specs)
    ]
    return pl.pallas_call(
        kernel,
        out_shape=out_memory(*out_shape) if out_memory else jax.ShapeDtypeStruct(*out_shape),
        in_specs=in_specs,
        out_specs=VMEM,
        scratch_shapes=list(scratch),
    )(*args)


def split(v):
    high = v.astype(BF16)
    return high, (v - high.astype(F32)).astype(BF16)


def iota(shape, axis):
    return lax.broadcasted_iota(jnp.int32, shape, axis)


def select_kernel(index_ref, hidden_ref, out_ref):
    chosen = jnp.where(iota((256, 64), 0) == index_ref[...], 1.0, 0.0).astype(BF16)
    picked = lax.dot_general(
        chosen, hidden_ref[...], (((0,), (0,)), ((), ())), preferred_element_type=F32
    ).astype(BF16)
    for i in range(8):
        out_ref[i] = picked


def logits_kernel(core_ref, own_ref, other_ref, head_ref, out_ref, held_ref, sems):
    copies = [
        pltpu.make_async_copy(head_ref.at[:, pl.ds(n * 256, 256)], held_ref.at[n], sems.at[n]) for n in range(6)
    ]
    for copy in copies:
        copy.start()
    first = core_ref[0] == 0
    lhs = []
    for group in range(8 // G):
        rows = pl.ds(group * LANES, LANES)
        features = []
        for x in range(4):
            own, other = own_ref[x, rows, :], other_ref[x, rows, :]
            features.append(jnp.where(first, own, other))
            features.append(jnp.where(first, other, own))
        lhs.append(jnp.concatenate(features, axis=1))
    for n in range(6):
        copies[n].wait()
        for group in range(8 // G):
            part = jnp.dot(lhs[group], held_ref[n], preferred_element_type=F32).astype(BF16)
            for t in range(2):
                piece, lane = divmod((2 * n + t) * 128, PART)
                out_ref[group * G + piece, :, pl.ds(lane, 128)] = part[:, t * 128 : (t + 1) * 128]


def project_kernel(parts_ref, basis_ref, out_ref):
    logits = parts_ref[0].astype(F32)
    for i in range(1, 8):
        logits = logits + parts_ref[i].astype(F32)
    top_high, top_low = split(jnp.max(logits, axis=1, keepdims=True))
    top_high, top_low = top_high.astype(F32), top_low.astype(F32)
    weights = jnp.exp(logits - (top_high + top_low))
    den_high, den_low = split(jnp.sum(weights, axis=1, keepdims=True))
    wei_high, wei_low = split(jnp.sum(weights * logits, axis=1, keepdims=True))
    lane = iota((LANES, 128), 1)
    stats = jnp.zeros((LANES, 128), F32)
    for i, v in enumerate([top_high, top_low, den_high, den_low, wei_high, wei_low]):
        stats = jnp.where(lane == i, v.astype(F32), stats)
    stats = stats.T[0:16, :]
    high, low = split(logits)
    lhs = jnp.concatenate([high, low, jnp.ones((128, PART), BF16)], axis=0)
    lane = iota((16, 128), 1)
    spread = []
    for j in range(4):
        rhs = jnp.concatenate([basis_ref[2 * j], basis_ref[2 * j + 1]], axis=1)
        both = jnp.dot(lhs, rhs, preferred_element_type=F32)
        turned = (both[0:LANES] + both[LANES : 2 * LANES]).T.astype(BF16)
        sums = both[2 * LANES : 2 * LANES + 128].T
        for half in range(2):
            y = 2 * j + half
            line = jnp.zeros((16, 128), F32)
            for block in range(8):
                start = half * 128 + block * 16
                out_ref[block, y * 16 : y * 16 + 16, :] = turned[start : start + 16]
                line = jnp.where(lane == block, sums[start : start + 16], line)
            spread.append(line)
    sums = jnp.concatenate(spread, axis=0).T
    row = iota((16, LANES), 0)
    for block in range(8):
        sums_high, sums_low = split(sums[block : block + 1])
        extra = jnp.where(row < 6, stats, 0.0)
        if LANES > 128:
            zero = jnp.zeros((1, LANES - 128), BF16)
            sums_high = jnp.concatenate([sums_high, zero], axis=1)
            sums_low = jnp.concatenate([sums_low, zero], axis=1)
        extra = jnp.where(row == 6, sums_high.astype(F32), extra)
        extra = jnp.where(row == 7, sums_low.astype(F32), extra)
        out_ref[block, 128:144, :] = extra.astype(BF16)


def merge(tiles):
    tops = [t[0:1] + t[1:2] for t in tiles]
    top = tops[0]
    for t in tops[1:]:
        top = jnp.maximum(top, t)
    denominator, weighted, sums = 0.0, 0.0, 0.0
    for mine, tile in zip(tops, tiles):
        scale = jnp.exp(mine - top)
        denominator = denominator + scale * (tile[2:3] + tile[3:4])
        weighted = weighted + scale * (tile[4:5] + tile[5:6])
        sums = sums + (tile[6:7] + tile[7:8])
    return top, denominator, weighted, sums


def chip_kernel(in_ref, out_ref):
    total = in_ref[0, 0:128, :].astype(F32)
    for i in range(1, 8):
        total = total + in_ref[i, 0:128, :].astype(F32)
    top, denominator, weighted, sums = merge([in_ref[i, 128:144, :].astype(F32) for i in range(8)])
    pairs = [h for v in (top, denominator, weighted) for h in split(v)]
    sums_high, sums_low = split(sums[:, 0:128])
    sums_high, sums_low = sums_high.astype(F32), sums_low.astype(F32)
    row, lane = iota((16, 128), 0), iota((16, 128), 1)
    for owner in range(G):
        lanes = slice((owner // 2) * 128, (owner // 2) * 128 + 128)
        stats = jnp.zeros((16, 128), F32)
        for i, v in enumerate(pairs):
            stats = jnp.where(row == i, v[:, lanes].astype(F32), stats)
        if owner % 2 == 0:
            stats = pltpu.roll(stats, 64, 1)
        for y in range(8):
            block = total[y * 16 : y * 16 + 16, lanes]
            if owner % 2:
                block = pltpu.roll(block, 64, 1)
            shift = (64 - 16 * y) % 128
            line_high = pltpu.roll(jnp.broadcast_to(sums_high, (8, 128)), shift, 1)[0:1]
            line_low = pltpu.roll(jnp.broadcast_to(sums_low, (8, 128)), shift, 1)[0:1]
            extra = jnp.where(row == 6, line_high, jnp.where(row == 7, line_low, stats))
            out_ref[y * G + owner] = jnp.where(lane < 64, block, extra).astype(BF16)


def finish_kernel(count_ref, in_ref, out_ref):
    tiles = [in_ref[i].astype(F32) for i in range(8 * G)]
    total = tiles[0]
    for t in tiles[1:]:
        total = total + t
    _, denominator, weighted, sums = merge(tiles)
    expected = pltpu.roll(jnp.broadcast_to(weighted / denominator, (8, 128)), 64, 1)[0:1]
    row, lane = iota((16, 128), 0), iota((16, 128), 1)
    column = jnp.sum(jnp.where(lane == row + 64, sums, 0.0), axis=1, keepdims=True)
    result = jnp.where(lane < count_ref[0], total - expected * column, 0.0)
    out_ref[...] = result[:, 0:64]


def shards(hidden, head_weight, vocab_basis, keep_index, counts):
    def exchange(v, axes):
        return lax.all_to_all(v, axes, 0, 0, tiled=True)

    core = lax.axis_index("c").astype(jnp.int32).reshape(1)
    basis_parts = jnp.broadcast_to(vocab_basis.reshape(1, G, PART, 128), (8 // G, G, PART, 128))
    basis = exchange(basis_parts.reshape(8, PART, 128), Z)
    owned = call(select_kernel, ((8, 64, 128), BF16), [OUTER, OUTER], keep_index.reshape(1, 64), hidden)
    sliced = exchange(exchange(owned, "y"), Z)
    mine = exchange(jnp.broadcast_to(sliced.reshape(1, 512, 128), (4, 512, 128)), "x")
    theirs = lax.ppermute(mine, "c", [(0, 1), (1, 0)])
    parts = call(
        logits_kernel,
        ((8, LANES, PART), BF16),
        [SMEM, VMEM, VMEM, STAY],
        core,
        mine,
        theirs,
        head_weight,
        scratch=[pltpu.VMEM((6, 1024, 256), BF16), pltpu.SemaphoreType.DMA((6,))],
    )
    sums = call(project_kernel, ((8, 144, LANES), BF16), [VMEM, VMEM], exchange(parts, Z), basis)
    sums = call(chip_kernel, ((8 * G, 16, 128), BF16), [VMEM], exchange(sums, ("x", "c")))
    sums = exchange(sums, ("y", "zl"))
    return call(finish_kernel, ((16, 64), F32), [SMEM, VMEM], counts, sums, out_memory=None).T


def solution(mesh):
    grid = Mesh(mesh.devices.reshape(8 // G, G, 8, 4, 2), ALL)
    rows, cols = ("zh", "zl"), ("y", "x", "c")
    in_specs = (P(rows, cols), P(rows, cols), P(cols, rows), P(rows), P(rows))
    return jax.shard_map(shards, mesh=grid, in_specs=in_specs, out_specs=P(rows, cols), check_vma=False)
```

```python
import jax
import jax.numpy as jnp
from jax import lax
from jax.experimental import pallas as pl
from jax.experimental.pallas import tpu as pltpu
from jax.sharding import Mesh, PartitionSpec as P


F32 = jnp.float32
BF16 = jnp.bfloat16
ALL = ("z", "y", "x", "c")
VMEM = pl.BlockSpec(memory_space=pltpu.VMEM)
SMEM = pl.BlockSpec(memory_space=pltpu.SMEM)
OUTER = pl.BlockSpec(memory_space=pltpu.VMEM)
STAY = pl.BlockSpec(memory_space=pl.ANY)


def call(kernel, out_shape, in_specs, *args, scratch=(), out_memory=pltpu.VMEM):
    args = [
        pltpu.with_memory_space_constraint(a, pltpu.VMEM) if spec is VMEM else a
        for a, spec in zip(args, in_specs)
    ]
    return pl.pallas_call(
        kernel,
        out_shape=out_memory(*out_shape) if out_memory else jax.ShapeDtypeStruct(*out_shape),
        in_specs=in_specs,
        out_specs=VMEM,
        scratch_shapes=list(scratch),
    )(*args)


def split(v):
    high = v.astype(BF16)
    return high, (v - high.astype(F32)).astype(BF16)


def iota(shape, axis):
    return lax.broadcasted_iota(jnp.int32, shape, axis)


def select_kernel(index_ref, hidden_ref, out_ref):
    chosen = jnp.where(iota((256, 64), 0) == index_ref[...], 1.0, 0.0).astype(BF16)
    picked = lax.dot_general(
        chosen, hidden_ref[...], (((0,), (0,)), ((), ())), preferred_element_type=F32
    ).astype(BF16)
    for i in range(8):
        out_ref[i] = picked


def logits_kernel(core_ref, own_ref, other_ref, head_ref, out_ref, held_ref, sems):
    copies = [
        pltpu.make_async_copy(head_ref.at[:, pl.ds(n * 256, 256)], held_ref.at[n], sems.at[n]) for n in range(6)
    ]
    for copy in copies:
        copy.start()
    first = core_ref[0] == 0
    features = []
    for x in range(4):
        own, other = own_ref[x], other_ref[x]
        features.append(jnp.where(first, own, other))
        features.append(jnp.where(first, other, own))
    lhs = jnp.concatenate(features, axis=1)
    for n in range(6):
        copies[n].wait()
        part = jnp.dot(lhs, held_ref[n], preferred_element_type=F32).astype(BF16)
        for owner in range(8):
            out_ref[owner, :, pl.ds(n * 256, 256)] = part[owner * 64 : owner * 64 + 64]


def project_kernel(parts_ref, basis_ref, out_ref, held_ref, sems):
    copies = [
        pltpu.make_async_copy(basis_ref.at[pl.ds(2 * j, 2)], held_ref.at[j], sems.at[j]) for j in range(4)
    ]
    for copy in copies:
        copy.start()
    logits = parts_ref[0].astype(F32)
    for i in range(1, 8):
        logits = logits + parts_ref[i].astype(F32)
    top_high, top_low = split(jnp.max(logits, axis=1, keepdims=True))
    top_high, top_low = top_high.astype(F32), top_low.astype(F32)
    weights = jnp.exp(logits - (top_high + top_low))
    den_high, den_low = split(jnp.sum(weights, axis=1, keepdims=True))
    wei_high, wei_low = split(jnp.sum(weights * logits, axis=1, keepdims=True))
    lane = iota((64, 128), 1)
    stats = jnp.zeros((64, 128), F32)
    for i, v in enumerate([top_high, top_low, den_high, den_low, wei_high, wei_low]):
        stats = jnp.where(lane == i, v.astype(F32), stats)
    stats = jnp.concatenate([jnp.zeros((64, 128), F32), stats], axis=0).T[0:16, :]
    high, low = split(logits)
    lhs = jnp.concatenate([high, low, jnp.ones((128, 1536), BF16)], axis=0)
    row, lane = iota((16, 128), 0), iota((16, 128), 1)
    for j in range(4):
        copies[j].wait()
        rhs = jnp.concatenate([held_ref[j, 0], held_ref[j, 1]], axis=1)
        both = jnp.dot(lhs, rhs, preferred_element_type=F32)
        turned = jnp.concatenate([both[0:64] + both[64:128], jnp.zeros((64, 256), F32)], axis=0).T
        for half in range(2):
            sums_high, sums_low = split(both[128:136, half * 128 : half * 128 + 128])
            sums_high, sums_low = sums_high.astype(F32), sums_low.astype(F32)
            for block in range(8):
                start = half * 128 + block * 16
                shift = (64 - 16 * block) % 128
                line_high = pltpu.roll(sums_high, shift, 1)[0:1]
                line_low = pltpu.roll(sums_low, shift, 1)[0:1]
                extra = jnp.where(row == 6, line_high, jnp.where(row == 7, line_low, stats))
                tile = jnp.where(lane < 64, turned[start : start + 16], extra)
                out_ref[16 * j + 8 * half + block] = tile.astype(BF16)


def merge(tiles):
    tops = [t[0:1] + t[1:2] for t in tiles]
    top = tops[0]
    for t in tops[1:]:
        top = jnp.maximum(top, t)
    denominator, weighted, sums = 0.0, 0.0, 0.0
    for mine, tile in zip(tops, tiles):
        scale = jnp.exp(mine - top)
        denominator = denominator + scale * (tile[2:3] + tile[3:4])
        weighted = weighted + scale * (tile[4:5] + tile[5:6])
        sums = sums + (tile[6:7] + tile[7:8])
    return top, denominator, weighted, sums


def finish_kernel(count_ref, in_ref, out_ref):
    tiles = [in_ref[i].astype(F32) for i in range(64)]
    total = tiles[0]
    for t in tiles[1:]:
        total = total + t
    _, denominator, weighted, sums = merge(tiles)
    expected = pltpu.roll(jnp.broadcast_to(weighted / denominator, (8, 128)), 64, 1)[0:1]
    row, lane = iota((16, 128), 0), iota((16, 128), 1)
    column = jnp.sum(jnp.where(lane == row + 64, sums, 0.0), axis=1, keepdims=True)
    result = jnp.where(lane < count_ref[0], total - expected * column, 0.0)
    out_ref[...] = result[:, 0:64]


def shards(hidden, head_weight, vocab_basis, keep_index, counts):
    def exchange(v, axes):
        return lax.all_to_all(v, axes, 0, 0, tiled=True)

    core = lax.axis_index("c").astype(jnp.int32).reshape(1)
    basis = lax.all_gather(vocab_basis, "z")
    owned = call(select_kernel, ((8, 64, 128), BF16), [OUTER, OUTER], keep_index.reshape(1, 64), hidden)
    sliced = exchange(exchange(owned, "y"), "z")
    mine = exchange(jnp.broadcast_to(sliced.reshape(1, 512, 128), (4, 512, 128)), "x")
    theirs = lax.ppermute(mine, "c", [(0, 1), (1, 0)])
    parts = call(
        logits_kernel,
        ((8, 64, 1536), BF16),
        [SMEM, VMEM, VMEM, STAY],
        core,
        mine,
        theirs,
        head_weight,
        scratch=[pltpu.VMEM((6, 1024, 256), BF16), pltpu.SemaphoreType.DMA((6,))],
    )
    tiles = call(
        project_kernel,
        ((64, 16, 128), BF16),
        [VMEM, STAY],
        exchange(parts, "z"),
        basis,
        scratch=[pltpu.VMEM((4, 2, 1536, 128), BF16), pltpu.SemaphoreType.DMA((4,))],
    )
    tiles = exchange(tiles, ("y", "x", "c"))
    return call(finish_kernel, ((16, 64), F32), [SMEM, VMEM], counts, tiles, out_memory=None).T


def solution(mesh):
    grid = Mesh(mesh.devices.reshape(8, 8, 4, 2), ALL)
    rows, cols = "z", ("y", "x", "c")
    in_specs = (P(rows, cols), P(rows, cols), P(cols, rows), P(rows), P(rows))
    return jax.shard_map(shards, mesh=grid, in_specs=in_specs, out_specs=P(rows, cols), check_vma=False)
```

```python
import jax
import jax.numpy as jnp
from jax import lax
from jax.experimental import pallas as pl
from jax.experimental.pallas import tpu as pltpu
from jax.sharding import Mesh, PartitionSpec as P


F32 = jnp.float32
BF16 = jnp.bfloat16
ALL = ("z", "y", "x", "c")
VMEM = pl.BlockSpec(memory_space=pltpu.VMEM)
SMEM = pl.BlockSpec(memory_space=pltpu.SMEM)
OUTER = pl.BlockSpec(memory_space=pltpu.VMEM)
STAY = pl.BlockSpec(memory_space=pl.ANY)


def call(kernel, out_shape, in_specs, *args, scratch=(), out_memory=pltpu.VMEM):
    args = [
        pltpu.with_memory_space_constraint(a, pltpu.VMEM) if spec is VMEM else a
        for a, spec in zip(args, in_specs)
    ]
    return pl.pallas_call(
        kernel,
        out_shape=out_memory(*out_shape) if out_memory else jax.ShapeDtypeStruct(*out_shape),
        in_specs=in_specs,
        out_specs=VMEM,
        scratch_shapes=list(scratch),
    )(*args)


def split(v):
    high = v.astype(BF16)
    return high, (v - high.astype(F32)).astype(BF16)


def iota(shape, axis):
    return lax.broadcasted_iota(jnp.int32, shape, axis)


def select_kernel(index_ref, hidden_ref, out_ref):
    chosen = jnp.where(iota((256, 64), 0) == index_ref[...], 1.0, 0.0).astype(BF16)
    out_ref[...] = lax.dot_general(
        chosen, hidden_ref[...], (((0,), (0,)), ((), ())), preferred_element_type=F32
    ).astype(BF16)


def logits_kernel(core_ref, own_ref, other_ref, head_ref, out_ref, held_ref, sems):
    copies = [
        pltpu.make_async_copy(head_ref.at[:, pl.ds(n * 256, 256)], held_ref.at[n], sems.at[n]) for n in range(6)
    ]
    for copy in copies:
        copy.start()
    first = core_ref[0] == 0
    lhs = []
    for group in range(2):
        rows = pl.ds(group * 256, 256)
        features = []
        for x in range(4):
            picks = [16 * group + 4 * o + x for o in range(4)]
            own = jnp.concatenate([own_ref[p] for p in picks], axis=0)
            other = jnp.concatenate([other_ref[p] for p in picks], axis=0)
            features.append(jnp.where(first, own, other))
            features.append(jnp.where(first, other, own))
        lhs.append(jnp.concatenate(features, axis=1))
    for n in range(6):
        copies[n].wait()
        for group in range(2):
            part = jnp.dot(lhs[group], held_ref[n], preferred_element_type=F32).astype(BF16)
            for owner in range(4):
                out_ref[group * 4 + owner, :, pl.ds(n * 256, 256)] = part[owner * 64 : owner * 64 + 64]


def project_kernel(parts_ref, basis_ref, out_ref, held_ref, sems):
    copies = [
        pltpu.make_async_copy(basis_ref.at[pl.ds(2 * j, 2)], held_ref.at[j], sems.at[j]) for j in range(4)
    ]
    for copy in copies:
        copy.start()
    logits = parts_ref[0].astype(F32)
    for i in range(1, 8):
        logits = logits + parts_ref[i].astype(F32)
    top_high, top_low = split(jnp.max(logits, axis=1, keepdims=True))
    top_high, top_low = top_high.astype(F32), top_low.astype(F32)
    weights = jnp.exp(logits - (top_high + top_low))
    den_high, den_low = split(jnp.sum(weights, axis=1, keepdims=True))
    wei_high, wei_low = split(jnp.sum(weights * logits, axis=1, keepdims=True))
    lane = iota((64, 128), 1)
    stats = jnp.zeros((64, 128), F32)
    for i, v in enumerate([top_high, top_low, den_high, den_low, wei_high, wei_low]):
        stats = jnp.where(lane == i, v.astype(F32), stats)
    stats = jnp.concatenate([jnp.zeros((64, 128), F32), stats], axis=0).T[0:16, :]
    high, low = split(logits)
    lhs = jnp.concatenate([high, low, jnp.ones((16, 1536), BF16)], axis=0)
    row, lane = iota((16, 128), 0), iota((16, 128), 1)
    for j in range(4):
        copies[j].wait()
        rhs = jnp.concatenate([held_ref[j, 0], held_ref[j, 1]], axis=1)
        both = jnp.dot(lhs, rhs, preferred_element_type=F32)
        turned = jnp.concatenate([both[0:64] + both[64:128], jnp.zeros((64, 256), F32)], axis=0).T
        for half in range(2):
            sums_high, sums_low = split(both[128:136, half * 128 : half * 128 + 128])
            sums_high, sums_low = sums_high.astype(F32), sums_low.astype(F32)
            for block in range(8):
                start = half * 128 + block * 16
                shift = (64 - 16 * block) % 128
                line_high = pltpu.roll(sums_high, shift, 1)[0:1]
                line_low = pltpu.roll(sums_low, shift, 1)[0:1]
                extra = jnp.where(row == 6, line_high, jnp.where(row == 7, line_low, stats))
                tile = jnp.where(lane < 64, turned[start : start + 16], extra)
                out_ref[16 * j + 8 * half + block] = tile.astype(BF16)


def merge(tiles):
    tops = [t[0:1] + t[1:2] for t in tiles]
    top = tops[0]
    for t in tops[1:]:
        top = jnp.maximum(top, t)
    denominator, weighted, sums = 0.0, 0.0, 0.0
    for mine, tile in zip(tops, tiles):
        scale = jnp.exp(mine - top)
        denominator = denominator + scale * (tile[2:3] + tile[3:4])
        weighted = weighted + scale * (tile[4:5] + tile[5:6])
        sums = sums + (tile[6:7] + tile[7:8])
    return top, denominator, weighted, sums


def finish_kernel(count_ref, in_ref, out_ref):
    tiles = [in_ref[i].astype(F32) for i in range(64)]
    total = tiles[0]
    for t in tiles[1:]:
        total = total + t
    _, denominator, weighted, sums = merge(tiles)
    expected = pltpu.roll(jnp.broadcast_to(weighted / denominator, (8, 128)), 64, 1)[0:1]
    row, lane = iota((16, 128), 0), iota((16, 128), 1)
    column = jnp.sum(jnp.where(lane == row + 64, sums, 0.0), axis=1, keepdims=True)
    result = jnp.where(lane < count_ref[0], total - expected * column, 0.0)
    out_ref[...] = result[:, 0:64]


def shards(hidden, head_weight, vocab_basis, keep_index, counts):
    def exchange(v, axes):
        return lax.all_to_all(v, axes, 0, 0, tiled=True)

    core = lax.axis_index("c").astype(jnp.int32).reshape(1)
    basis = lax.all_gather(vocab_basis, "z")
    owned = call(select_kernel, ((64, 128), BF16), [OUTER, OUTER], keep_index.reshape(1, 64), hidden)
    pairs = [((z * 8 + y) * 8 + k, (y * 8 + z) * 8 + k) for z in range(8) for y in range(8) for k in range(8)]
    moved = lax.ppermute(owned, ("z", "y", "x", "c"), pairs)
    mine = exchange(jnp.broadcast_to(moved[None], (32, 64, 128)), ("y", "x"))
    theirs = lax.ppermute(mine, "c", [(0, 1), (1, 0)])
    parts = call(
        logits_kernel,
        ((8, 64, 1536), BF16),
        [SMEM, VMEM, VMEM, STAY],
        core,
        mine,
        theirs,
        head_weight,
        scratch=[pltpu.VMEM((6, 1024, 256), BF16), pltpu.SemaphoreType.DMA((6,))],
    )
    tiles = call(
        project_kernel,
        ((64, 16, 128), BF16),
        [VMEM, STAY],
        exchange(parts, "z"),
        basis,
        scratch=[pltpu.VMEM((4, 2, 1536, 128), BF16), pltpu.SemaphoreType.DMA((4,))],
    )
    tiles = exchange(tiles, ("y", "x", "c"))
    return call(finish_kernel, ((16, 64), F32), [SMEM, VMEM], counts, tiles, out_memory=None).T


def solution(mesh):
    grid = Mesh(mesh.devices.reshape(8, 8, 4, 2), ALL)
    rows, cols = "z", ("y", "x", "c")
    in_specs = (P(rows, cols), P(rows, cols), P(cols, rows), P(rows), P(rows))
    return jax.shard_map(shards, mesh=grid, in_specs=in_specs, out_specs=P(rows, cols), check_vma=False)
```

```python
import jax
import jax.numpy as jnp
from jax import lax
from jax.experimental import pallas as pl
from jax.experimental.pallas import tpu as pltpu
from jax.sharding import Mesh, PartitionSpec as P


F32 = jnp.float32
BF16 = jnp.bfloat16
ALL = ("z", "y", "x", "c")
VMEM = pl.BlockSpec(memory_space=pltpu.VMEM)
SMEM = pl.BlockSpec(memory_space=pltpu.SMEM)
OUTER = pl.BlockSpec(memory_space=pltpu.VMEM)
STAY = pl.BlockSpec(memory_space=pl.ANY)


def call(kernel, out_shape, in_specs, *args, scratch=(), out_memory=pltpu.VMEM):
    args = [
        pltpu.with_memory_space_constraint(a, pltpu.VMEM) if spec is VMEM else a
        for a, spec in zip(args, in_specs)
    ]
    if isinstance(out_shape, list):
        shapes = [pltpu.VMEM(*o) for o in out_shape]
    else:
        shapes = out_memory(*out_shape) if out_memory else jax.ShapeDtypeStruct(*out_shape)
    return pl.pallas_call(
        kernel,
        out_shape=shapes,
        in_specs=in_specs,
        out_specs=[VMEM] * len(out_shape) if isinstance(out_shape, list) else VMEM,
        scratch_shapes=list(scratch),
    )(*args)


def split(v):
    high = v.astype(BF16)
    return high, (v - high.astype(F32)).astype(BF16)


def iota(shape, axis):
    return lax.broadcasted_iota(jnp.int32, shape, axis)


def select_kernel(index_ref, hidden_ref, out_ref):
    chosen = jnp.where(iota((256, 64), 0) == index_ref[...], 1.0, 0.0).astype(BF16)
    out_ref[...] = lax.dot_general(
        chosen, hidden_ref[...], (((0,), (0,)), ((), ())), preferred_element_type=F32
    ).astype(BF16)


def logits_kernel(core_ref, own_ref, other_ref, head_ref, out_ref, held_ref, sems):
    copies = [
        pltpu.make_async_copy(head_ref.at[:, pl.ds(n * 256, 256)], held_ref.at[n], sems.at[n]) for n in range(6)
    ]
    for copy in copies:
        copy.start()
    first = core_ref[0] == 0
    lhs = []
    for group in range(2):
        rows = pl.ds(group * 256, 256)
        features = []
        for x in range(4):
            picks = [16 * group + 4 * o + x for o in range(4)]
            own = jnp.concatenate([own_ref[p] for p in picks], axis=0)
            other = jnp.concatenate([other_ref[p] for p in picks], axis=0)
            features.append(jnp.where(first, own, other))
            features.append(jnp.where(first, other, own))
        lhs.append(jnp.concatenate(features, axis=1))
    for n in range(6):
        copies[n].wait()
        for group in range(2):
            part = jnp.dot(lhs[group], held_ref[n], preferred_element_type=F32).astype(BF16)
            for owner in range(4):
                out_ref[group * 4 + owner, :, pl.ds(n * 256, 256)] = part[owner * 64 : owner * 64 + 64]


def project_kernel(core_ref, parts_ref, basis_ref, keep_ref, send_ref, held_ref, tiles_ref, sems):
    copies = [
        pltpu.make_async_copy(basis_ref.at[pl.ds(2 * j, 2)], held_ref.at[j], sems.at[j]) for j in range(4)
    ]
    for copy in copies:
        copy.start()
    logits = parts_ref[0].astype(F32)
    for i in range(1, 8):
        logits = logits + parts_ref[i].astype(F32)
    top_high, top_low = split(jnp.max(logits, axis=1, keepdims=True))
    top_high, top_low = top_high.astype(F32), top_low.astype(F32)
    weights = jnp.exp(logits - (top_high + top_low))
    den_high, den_low = split(jnp.sum(weights, axis=1, keepdims=True))
    wei_high, wei_low = split(jnp.sum(weights * logits, axis=1, keepdims=True))
    lane = iota((64, 128), 1)
    stats = jnp.zeros((64, 128), F32)
    for i, v in enumerate([top_high, top_low, den_high, den_low, wei_high, wei_low]):
        stats = jnp.where(lane == i, v.astype(F32), stats)
    stats = jnp.concatenate([jnp.zeros((64, 128), F32), stats], axis=0).T[0:16, :]
    high, low = split(logits)
    lhs = jnp.concatenate([high, low, jnp.ones((16, 1536), BF16)], axis=0)
    row, lane = iota((16, 128), 0), iota((16, 128), 1)
    for j in range(4):
        copies[j].wait()
        rhs = jnp.concatenate([held_ref[j, 0], held_ref[j, 1]], axis=1)
        both = jnp.dot(lhs, rhs, preferred_element_type=F32)
        turned = jnp.concatenate([both[0:64] + both[64:128], jnp.zeros((64, 256), F32)], axis=0).T
        for half in range(2):
            sums_high, sums_low = split(both[128:136, half * 128 : half * 128 + 128])
            sums_high, sums_low = sums_high.astype(F32), sums_low.astype(F32)
            for block in range(8):
                start = half * 128 + block * 16
                shift = (64 - 16 * block) % 128
                line_high = pltpu.roll(sums_high, shift, 1)[0:1]
                line_low = pltpu.roll(sums_low, shift, 1)[0:1]
                extra = jnp.where(row == 6, line_high, jnp.where(row == 7, line_low, stats))
                tile = jnp.where(lane < 64, turned[start : start + 16], extra)
                tiles_ref[block % 2, 8 * j + 4 * half + block // 2] = tile.astype(BF16)
    keep_ref[...] = tiles_ref[core_ref[0]]
    send_ref[...] = tiles_ref[1 - core_ref[0]]


def merge(tiles):
    tops = [t[0:1] + t[1:2] for t in tiles]
    top = tops[0]
    for t in tops[1:]:
        top = jnp.maximum(top, t)
    denominator, weighted, sums = 0.0, 0.0, 0.0
    for mine, tile in zip(tops, tiles):
        scale = jnp.exp(mine - top)
        denominator = denominator + scale * (tile[2:3] + tile[3:4])
        weighted = weighted + scale * (tile[4:5] + tile[5:6])
        sums = sums + (tile[6:7] + tile[7:8])
    return top, denominator, weighted, sums


def pair_kernel(keep_ref, recv_ref, out_ref):
    top, denominator, weighted, _ = merge([keep_ref[0].astype(F32), recv_ref[0].astype(F32)])
    row, lane = iota((16, 128), 0), iota((16, 128), 1)
    stats = jnp.zeros((16, 128), F32)
    for i, v in enumerate([h for v in (top, denominator, weighted) for h in split(v)]):
        stats = jnp.where(row == i, v.astype(F32), stats)
    shared = jnp.logical_and(lane >= 64, row < 6)
    for i in range(32):
        keep, recv = keep_ref[i].astype(F32), recv_ref[i].astype(F32)
        sums_high, sums_low = split((keep[6:7] + keep[7:8]) + (recv[6:7] + recv[7:8]))
        tile = jnp.where(row == 6, sums_high.astype(F32), sums_low.astype(F32))
        tile = jnp.where(jnp.logical_and(lane >= 64, row < 8), tile, keep + recv)
        out_ref[i] = jnp.where(shared, stats, tile).astype(BF16)


def finish_kernel(count_ref, in_ref, out_ref):
    tiles = [in_ref[i].astype(F32) for i in range(32)]
    total = tiles[0]
    for t in tiles[1:]:
        total = total + t
    _, denominator, weighted, sums = merge(tiles)
    expected = pltpu.roll(jnp.broadcast_to(weighted / denominator, (8, 128)), 64, 1)[0:1]
    row, lane = iota((16, 128), 0), iota((16, 128), 1)
    column = jnp.sum(jnp.where(lane == row + 64, sums, 0.0), axis=1, keepdims=True)
    result = jnp.where(lane < count_ref[0], total - expected * column, 0.0)
    out_ref[...] = result[:, 0:64]


def shards(hidden, head_weight, vocab_basis, keep_index, counts):
    def exchange(v, axes):
        return lax.all_to_all(v, axes, 0, 0, tiled=True)

    core = lax.axis_index("c").astype(jnp.int32).reshape(1)
    owned = call(select_kernel, ((64, 128), BF16), [OUTER, OUTER], keep_index.reshape(1, 64), hidden)
    late_basis, owned = lax.optimization_barrier((vocab_basis, owned))
    basis = lax.all_gather(late_basis, "z")
    pairs = [((z * 8 + y) * 8 + k, (y * 8 + z) * 8 + k) for z in range(8) for y in range(8) for k in range(8)]
    moved = lax.ppermute(owned, ("z", "y", "x", "c"), pairs)
    mine = exchange(jnp.broadcast_to(moved[None], (32, 64, 128)), ("y", "x"))
    theirs = lax.ppermute(mine, "c", [(0, 1), (1, 0)])
    parts = call(
        logits_kernel,
        ((8, 64, 1536), BF16),
        [SMEM, VMEM, VMEM, STAY],
        core,
        mine,
        theirs,
        head_weight,
        scratch=[pltpu.VMEM((6, 1024, 256), BF16), pltpu.SemaphoreType.DMA((6,))],
    )
    keep, send = call(
        project_kernel,
        [((32, 16, 128), BF16), ((32, 16, 128), BF16)],
        [SMEM, VMEM, STAY],
        core,
        exchange(parts, "z"),
        basis,
        scratch=[
            pltpu.VMEM((4, 2, 1536, 128), BF16),
            pltpu.VMEM((2, 32, 16, 128), BF16),
            pltpu.SemaphoreType.DMA((4,)),
        ],
    )
    tiles = call(pair_kernel, ((32, 16, 128), BF16), [VMEM, VMEM], keep, lax.ppermute(send, "c", [(0, 1), (1, 0)]))
    tiles = exchange(tiles, ("y", "x"))
    return call(finish_kernel, ((16, 64), F32), [SMEM, VMEM], counts, tiles, out_memory=None).T


def solution(mesh):
    grid = Mesh(mesh.devices.reshape(8, 8, 4, 2), ALL)
    rows, cols = "z", ("y", "x", "c")
    in_specs = (P(rows, cols), P(rows, cols), P(cols, rows), P(rows), P(rows))
    return jax.shard_map(shards, mesh=grid, in_specs=in_specs, out_specs=P(rows, cols), check_vma=False)
```

```python
import jax
import jax.numpy as jnp
from jax import lax
from jax.experimental import pallas as pl
from jax.experimental.pallas import tpu as pltpu
from jax.sharding import Mesh, PartitionSpec as P


F32 = jnp.float32
BF16 = jnp.bfloat16
ALL = ("z", "y", "x", "c")
VMEM = pl.BlockSpec(memory_space=pltpu.VMEM)
SMEM = pl.BlockSpec(memory_space=pltpu.SMEM)
OUTER = pl.BlockSpec(memory_space=pltpu.VMEM)
STAY = pl.BlockSpec(memory_space=pl.ANY)


def call(kernel, out_shape, in_specs, *args, scratch=(), out_memory=pltpu.VMEM, limit=None):
    args = [
        pltpu.with_memory_space_constraint(a, pltpu.VMEM) if spec is VMEM else a
        for a, spec in zip(args, in_specs)
    ]
    if isinstance(out_shape, list):
        shapes = [pltpu.VMEM(*o) for o in out_shape]
    else:
        shapes = out_memory(*out_shape) if out_memory else jax.ShapeDtypeStruct(*out_shape)
    return pl.pallas_call(
        kernel,
        out_shape=shapes,
        in_specs=in_specs,
        out_specs=[VMEM] * len(out_shape) if isinstance(out_shape, list) else VMEM,
        scratch_shapes=list(scratch),
        compiler_params=pltpu.CompilerParams(vmem_limit_bytes=limit),
    )(*args)


def split(v):
    high = v.astype(BF16)
    return high, (v - high.astype(F32)).astype(BF16)


def iota(shape, axis):
    return lax.broadcasted_iota(jnp.int32, shape, axis)


def select_kernel(index_ref, hidden_ref, out_ref):
    chosen = jnp.where(iota((256, 64), 0) == index_ref[...], 1.0, 0.0).astype(BF16)
    out_ref[...] = lax.dot_general(
        chosen, hidden_ref[...], (((0,), (0,)), ((), ())), preferred_element_type=F32
    ).astype(BF16)


def hold_kernel(head_ref, out_ref, sem):
    copy = pltpu.make_async_copy(head_ref, out_ref, sem)
    copy.start()
    copy.wait()


def logits_kernel(core_ref, own_ref, other_ref, head_ref, out_ref):
    first = core_ref[0] == 0
    lhs = []
    for group in range(2):
        rows = pl.ds(group * 256, 256)
        features = []
        for x in range(4):
            picks = [16 * group + 4 * o + x for o in range(4)]
            own = jnp.concatenate([own_ref[p] for p in picks], axis=0)
            other = jnp.concatenate([other_ref[p] for p in picks], axis=0)
            features.append(jnp.where(first, own, other))
            features.append(jnp.where(first, other, own))
        lhs.append(jnp.concatenate(features, axis=1))
    for n in range(6):
        for group in range(2):
            part = jnp.dot(lhs[group], head_ref[:, n * 256 : n * 256 + 256], preferred_element_type=F32).astype(BF16)
            for owner in range(4):
                out_ref[group * 4 + owner, :, pl.ds(n * 256, 256)] = part[owner * 64 : owner * 64 + 64]


def project_kernel(core_ref, parts_ref, basis_ref, keep_ref, send_ref, held_ref, tiles_ref, sems):
    copies = [
        pltpu.make_async_copy(basis_ref.at[pl.ds(2 * j, 2)], held_ref.at[j], sems.at[j]) for j in range(4)
    ]
    for copy in copies:
        copy.start()
    logits = parts_ref[0].astype(F32)
    for i in range(1, 8):
        logits = logits + parts_ref[i].astype(F32)
    top_high, top_low = split(jnp.max(logits, axis=1, keepdims=True))
    top_high, top_low = top_high.astype(F32), top_low.astype(F32)
    weights = jnp.exp(logits - (top_high + top_low))
    den_high, den_low = split(jnp.sum(weights, axis=1, keepdims=True))
    wei_high, wei_low = split(jnp.sum(weights * logits, axis=1, keepdims=True))
    lane = iota((64, 128), 1)
    stats = jnp.zeros((64, 128), F32)
    for i, v in enumerate([top_high, top_low, den_high, den_low, wei_high, wei_low]):
        stats = jnp.where(lane == i, v.astype(F32), stats)
    stats = jnp.concatenate([jnp.zeros((64, 128), F32), stats], axis=0).T[0:16, :]
    high, low = split(logits)
    lhs = jnp.concatenate([high, low, jnp.ones((16, 1536), BF16)], axis=0)
    row, lane = iota((16, 128), 0), iota((16, 128), 1)
    for j in range(4):
        copies[j].wait()
        rhs = jnp.concatenate([held_ref[j, 0], held_ref[j, 1]], axis=1)
        both = jnp.dot(lhs, rhs, preferred_element_type=F32)
        turned = jnp.concatenate([both[0:64] + both[64:128], jnp.zeros((64, 256), F32)], axis=0).T
        for half in range(2):
            sums_high, sums_low = split(both[128:136, half * 128 : half * 128 + 128])
            sums_high, sums_low = sums_high.astype(F32), sums_low.astype(F32)
            for block in range(8):
                start = half * 128 + block * 16
                shift = (64 - 16 * block) % 128
                line_high = pltpu.roll(sums_high, shift, 1)[0:1]
                line_low = pltpu.roll(sums_low, shift, 1)[0:1]
                extra = jnp.where(row == 6, line_high, jnp.where(row == 7, line_low, stats))
                tile = jnp.where(lane < 64, turned[start : start + 16], extra)
                tiles_ref[block % 2, 8 * j + 4 * half + block // 2] = tile.astype(BF16)
    keep_ref[...] = tiles_ref[core_ref[0]]
    send_ref[...] = tiles_ref[1 - core_ref[0]]


def merge(tiles):
    tops = [t[0:1] + t[1:2] for t in tiles]
    top = tops[0]
    for t in tops[1:]:
        top = jnp.maximum(top, t)
    denominator, weighted, sums = 0.0, 0.0, 0.0
    for mine, tile in zip(tops, tiles):
        scale = jnp.exp(mine - top)
        denominator = denominator + scale * (tile[2:3] + tile[3:4])
        weighted = weighted + scale * (tile[4:5] + tile[5:6])
        sums = sums + (tile[6:7] + tile[7:8])
    return top, denominator, weighted, sums


def pair_kernel(keep_ref, recv_ref, out_ref):
    top, denominator, weighted, _ = merge([keep_ref[0].astype(F32), recv_ref[0].astype(F32)])
    row, lane = iota((16, 128), 0), iota((16, 128), 1)
    stats = jnp.zeros((16, 128), F32)
    for i, v in enumerate([h for v in (top, denominator, weighted) for h in split(v)]):
        stats = jnp.where(row == i, v.astype(F32), stats)
    shared = jnp.logical_and(lane >= 64, row < 6)
    for i in range(32):
        keep, recv = keep_ref[i].astype(F32), recv_ref[i].astype(F32)
        sums_high, sums_low = split((keep[6:7] + keep[7:8]) + (recv[6:7] + recv[7:8]))
        tile = jnp.where(row == 6, sums_high.astype(F32), sums_low.astype(F32))
        tile = jnp.where(jnp.logical_and(lane >= 64, row < 8), tile, keep + recv)
        out_ref[i] = jnp.where(shared, stats, tile).astype(BF16)


def finish_kernel(count_ref, in_ref, out_ref):
    tiles = [in_ref[i].astype(F32) for i in range(32)]
    total = tiles[0]
    for t in tiles[1:]:
        total = total + t
    _, denominator, weighted, sums = merge(tiles)
    expected = pltpu.roll(jnp.broadcast_to(weighted / denominator, (8, 128)), 64, 1)[0:1]
    row, lane = iota((16, 128), 0), iota((16, 128), 1)
    column = jnp.sum(jnp.where(lane == row + 64, sums, 0.0), axis=1, keepdims=True)
    result = jnp.where(lane < count_ref[...], total - expected * column, 0.0)
    out_ref[...] = result[:, 0:64]


def shards(hidden, head_weight, vocab_basis, keep_index, counts):
    def exchange(v, axes):
        return lax.all_to_all(v, axes, 0, 0, tiled=True)

    core = lax.axis_index("c").astype(jnp.int32).reshape(1)
    owned = call(select_kernel, ((64, 128), BF16), [OUTER, OUTER], keep_index.reshape(1, 64), hidden)
    late_basis, owned = lax.optimization_barrier((vocab_basis, owned))
    basis = lax.all_gather(late_basis, "z")
    pairs = [((z * 8 + y) * 8 + k, (y * 8 + z) * 8 + k) for z in range(8) for y in range(8) for k in range(8)]
    moved = lax.ppermute(owned, ("z", "y", "x", "c"), pairs)
    mine = exchange(jnp.broadcast_to(moved[None], (32, 64, 128)), ("y", "x"))
    theirs = lax.ppermute(mine, "c", [(0, 1), (1, 0)])
    held = call(
        hold_kernel,
        ((1024, 1536), BF16),
        [STAY],
        head_weight,
        scratch=[pltpu.SemaphoreType.DMA],
        limit=58 << 20,
    )
    parts = call(
        logits_kernel,
        ((8, 64, 1536), BF16),
        [SMEM, VMEM, VMEM, VMEM],
        core,
        mine,
        theirs,
        held,
        limit=32 << 20,
    )
    keep, send = call(
        project_kernel,
        [((32, 16, 128), BF16), ((32, 16, 128), BF16)],
        [SMEM, VMEM, STAY],
        core,
        exchange(parts, "z"),
        basis,
        scratch=[
            pltpu.VMEM((4, 2, 1536, 128), BF16),
            pltpu.VMEM((2, 32, 16, 128), BF16),
            pltpu.SemaphoreType.DMA((4,)),
        ],
    )
    tiles = call(pair_kernel, ((32, 16, 128), BF16), [VMEM, VMEM], keep, lax.ppermute(send, "c", [(0, 1), (1, 0)]))
    tiles = exchange(tiles, ("y", "x"))
    return call(finish_kernel, ((16, 64), F32), [OUTER, VMEM], counts.reshape(1, 1), tiles, out_memory=None).T


def solution(mesh):
    grid = Mesh(mesh.devices.reshape(8, 8, 4, 2), ALL)
    rows, cols = "z", ("y", "x", "c")
    in_specs = (P(rows, cols), P(rows, cols), P(cols, rows), P(rows), P(rows))
    return jax.shard_map(shards, mesh=grid, in_specs=in_specs, out_specs=P(rows, cols), check_vma=False)
```

```python
import jax
import jax.numpy as jnp
from jax import lax
from jax.experimental import pallas as pl
from jax.experimental.pallas import tpu as pltpu
from jax.sharding import Mesh, PartitionSpec as P


F32 = jnp.float32
BF16 = jnp.bfloat16
ALL = ("z", "y", "x", "c")
VMEM = pl.BlockSpec(memory_space=pltpu.VMEM)
SMEM = pl.BlockSpec(memory_space=pltpu.SMEM)
OUTER = pl.BlockSpec(memory_space=pltpu.VMEM)
STAY = pl.BlockSpec(memory_space=pl.ANY)


def call(kernel, out_shape, in_specs, *args, scratch=(), out_memory=pltpu.VMEM, limit=None):
    args = [
        pltpu.with_memory_space_constraint(a, pltpu.VMEM) if spec is VMEM else a
        for a, spec in zip(args, in_specs)
    ]
    if isinstance(out_shape, list):
        shapes = [pltpu.VMEM(*o) for o in out_shape]
    else:
        shapes = out_memory(*out_shape) if out_memory else jax.ShapeDtypeStruct(*out_shape)
    return pl.pallas_call(
        kernel,
        out_shape=shapes,
        in_specs=in_specs,
        out_specs=[VMEM] * len(out_shape) if isinstance(out_shape, list) else VMEM,
        scratch_shapes=list(scratch),
        compiler_params=pltpu.CompilerParams(vmem_limit_bytes=limit),
    )(*args)


def split(v):
    high = v.astype(BF16)
    return high, (v - high.astype(F32)).astype(BF16)


def iota(shape, axis):
    return lax.broadcasted_iota(jnp.int32, shape, axis)


def select_kernel(index_ref, hidden_ref, out_ref):
    chosen = jnp.where(iota((256, 64), 0) == index_ref[...], 1.0, 0.0).astype(BF16)
    out_ref[...] = lax.dot_general(
        chosen, hidden_ref[...], (((0,), (0,)), ((), ())), preferred_element_type=F32
    ).astype(BF16)


def hold_kernel(head_ref, count_ref, out_ref, live_ref, sem):
    live_ref[...] = jnp.broadcast_to(count_ref[...], (8, 128))
    copy = pltpu.make_async_copy(head_ref, out_ref, sem)
    copy.start()
    copy.wait()


def logits_kernel(core_ref, own_ref, other_ref, head_ref, out_ref):
    first = core_ref[0] == 0
    lhs = []
    for group in range(2):
        rows = pl.ds(group * 256, 256)
        features = []
        for x in range(4):
            picks = [16 * (1 - group) + 4 * o + x for o in range(4)]
            own = jnp.concatenate([own_ref[p] for p in picks], axis=0)
            other = jnp.concatenate([other_ref[p] for p in picks], axis=0)
            features.append(jnp.where(first, own, other))
            features.append(jnp.where(first, other, own))
        lhs.append(jnp.concatenate(features, axis=1))
    for n in range(6):
        for group in range(2):
            part = jnp.dot(lhs[group], head_ref[:, n * 256 : n * 256 + 256], preferred_element_type=F32).astype(BF16)
            for owner in range(4):
                out_ref[group * 4 + owner, :, pl.ds(n * 256, 256)] = part[owner * 64 : owner * 64 + 64]


def project_kernel(core_ref, parts_ref, basis_ref, keep_ref, send_ref, held_ref, tiles_ref, sems):
    copies = [
        pltpu.make_async_copy(basis_ref.at[pl.ds(2 * j, 2)], held_ref.at[j], sems.at[j]) for j in range(4)
    ]
    for copy in copies:
        copy.start()
    logits = parts_ref[0].astype(F32)
    for i in range(1, 8):
        logits = logits + parts_ref[i].astype(F32)
    top_high, top_low = split(jnp.max(logits, axis=1, keepdims=True))
    top_high, top_low = top_high.astype(F32), top_low.astype(F32)
    weights = jnp.exp(logits - (top_high + top_low))
    den_high, den_low = split(jnp.sum(weights, axis=1, keepdims=True))
    wei_high, wei_low = split(jnp.sum(weights * logits, axis=1, keepdims=True))
    lane = iota((64, 128), 1)
    stats = jnp.zeros((64, 128), F32)
    for i, v in enumerate([top_high, top_low, den_high, den_low, wei_high, wei_low]):
        stats = jnp.where(lane == i, v.astype(F32), stats)
    stats = jnp.concatenate([jnp.zeros((64, 128), F32), stats], axis=0).T[0:16, :]
    high, low = split(logits)
    lhs = jnp.concatenate([high, low, jnp.ones((16, 1536), BF16)], axis=0)
    row, lane = iota((16, 128), 0), iota((16, 128), 1)
    for j in range(4):
        copies[j].wait()
        rhs = jnp.concatenate([held_ref[j, 0], held_ref[j, 1]], axis=1)
        both = jnp.dot(lhs, rhs, preferred_element_type=F32)
        turned = jnp.concatenate([both[0:64] + both[64:128], jnp.zeros((64, 256), F32)], axis=0).T
        for half in range(2):
            sums_high, sums_low = split(both[128:136, half * 128 : half * 128 + 128])
            sums_high, sums_low = sums_high.astype(F32), sums_low.astype(F32)
            for block in range(8):
                start = half * 128 + block * 16
                shift = (64 - 16 * block) % 128
                line_high = pltpu.roll(sums_high, shift, 1)[0:1]
                line_low = pltpu.roll(sums_low, shift, 1)[0:1]
                extra = jnp.where(row == 6, line_high, jnp.where(row == 7, line_low, stats))
                tile = jnp.where(lane < 64, turned[start : start + 16], extra)
                tiles_ref[block % 2, 8 * j + 4 * half + block // 2] = tile.astype(BF16)
    keep_ref[...] = tiles_ref[core_ref[0]]
    send_ref[...] = tiles_ref[1 - core_ref[0]]


def merge(tiles):
    tops = [t[0:1] + t[1:2] for t in tiles]
    top = tops[0]
    for t in tops[1:]:
        top = jnp.maximum(top, t)
    denominator, weighted, sums = 0.0, 0.0, 0.0
    for mine, tile in zip(tops, tiles):
        scale = jnp.exp(mine - top)
        denominator = denominator + scale * (tile[2:3] + tile[3:4])
        weighted = weighted + scale * (tile[4:5] + tile[5:6])
        sums = sums + (tile[6:7] + tile[7:8])
    return top, denominator, weighted, sums


def pair_kernel(keep_ref, recv_ref, out_ref):
    top, denominator, weighted, _ = merge([keep_ref[0].astype(F32), recv_ref[0].astype(F32)])
    row, lane = iota((16, 128), 0), iota((16, 128), 1)
    stats = jnp.zeros((16, 128), F32)
    for i, v in enumerate([h for v in (top, denominator, weighted) for h in split(v)]):
        stats = jnp.where(row == i, v.astype(F32), stats)
    shared = jnp.logical_and(lane >= 64, row < 6)
    for i in range(32):
        keep, recv = keep_ref[i].astype(F32), recv_ref[i].astype(F32)
        sums_high, sums_low = split((keep[6:7] + keep[7:8]) + (recv[6:7] + recv[7:8]))
        tile = jnp.where(row == 6, sums_high.astype(F32), sums_low.astype(F32))
        tile = jnp.where(jnp.logical_and(lane >= 64, row < 8), tile, keep + recv)
        out_ref[i] = jnp.where(shared, stats, tile).astype(BF16)


def finish_kernel(count_ref, in_ref, out_ref):
    tiles = [in_ref[i].astype(F32) for i in range(32)]
    total = tiles[0]
    for t in tiles[1:]:
        total = total + t
    _, denominator, weighted, sums = merge(tiles)
    expected = pltpu.roll(jnp.broadcast_to(weighted / denominator, (8, 128)), 64, 1)[0:1]
    row, lane = iota((16, 128), 0), iota((16, 128), 1)
    column = jnp.sum(jnp.where(lane == row + 64, sums, 0.0), axis=1, keepdims=True)
    result = jnp.where(lane < count_ref[0:1, :], total - expected * column, 0.0)
    out_ref[...] = result[:, 0:64]


def shards(hidden, head_weight, vocab_basis, keep_index, counts):
    def exchange(v, axes):
        return lax.all_to_all(v, axes, 0, 0, tiled=True)

    core = lax.axis_index("c").astype(jnp.int32).reshape(1)
    owned = call(select_kernel, ((64, 128), BF16), [OUTER, OUTER], keep_index.reshape(1, 64), hidden)
    late_basis, owned = lax.optimization_barrier((vocab_basis, owned))
    basis = lax.all_gather(late_basis, "z")
    pairs = [((z * 8 + y) * 8 + k, (y * 8 + (z + 4) % 8) * 8 + k) for z in range(8) for y in range(8) for k in range(8)]
    moved = lax.ppermute(owned, ("z", "y", "x", "c"), pairs)
    mine = exchange(jnp.broadcast_to(moved[None], (32, 64, 128)), ("y", "x"))
    theirs = lax.ppermute(mine, "c", [(0, 1), (1, 0)])
    held, live = call(
        hold_kernel,
        [((1024, 1536), BF16), ((8, 128), jnp.int32)],
        [STAY, OUTER],
        head_weight,
        counts.reshape(1, 1),
        scratch=[pltpu.SemaphoreType.DMA],
        limit=58 << 20,
    )
    parts = call(
        logits_kernel,
        ((8, 64, 1536), BF16),
        [SMEM, VMEM, VMEM, VMEM],
        core,
        mine,
        theirs,
        held,
        limit=32 << 20,
    )
    keep, send = call(
        project_kernel,
        [((32, 16, 128), BF16), ((32, 16, 128), BF16)],
        [SMEM, VMEM, STAY],
        core,
        exchange(parts, "z"),
        basis,
        scratch=[
            pltpu.VMEM((4, 2, 1536, 128), BF16),
            pltpu.VMEM((2, 32, 16, 128), BF16),
            pltpu.SemaphoreType.DMA((4,)),
        ],
    )
    tiles = call(pair_kernel, ((32, 16, 128), BF16), [VMEM, VMEM], keep, lax.ppermute(send, "c", [(0, 1), (1, 0)]))
    tiles = exchange(tiles, ("y", "x"))
    return call(finish_kernel, ((16, 64), F32), [VMEM, VMEM], live, tiles, out_memory=None).T


def solution(mesh):
    grid = Mesh(mesh.devices.reshape(8, 8, 4, 2), ALL)
    rows, cols = "z", ("y", "x", "c")
    in_specs = (P(rows, cols), P(rows, cols), P(cols, rows), P(rows), P(rows))
    return jax.shard_map(shards, mesh=grid, in_specs=in_specs, out_specs=P(rows, cols), check_vma=False)
```

```python
import jax
import jax.numpy as jnp
from jax import lax
from jax.experimental import pallas as pl
from jax.experimental.pallas import tpu as pltpu
from jax.sharding import Mesh, PartitionSpec as P


F32 = jnp.float32
BF16 = jnp.bfloat16
ALL = ("z", "y", "x", "c")
VMEM = pl.BlockSpec(memory_space=pltpu.VMEM)
SMEM = pl.BlockSpec(memory_space=pltpu.SMEM)
OUTER = pl.BlockSpec(memory_space=pltpu.VMEM)
STAY = pl.BlockSpec(memory_space=pl.ANY)


def call(kernel, out_shape, in_specs, *args, scratch=(), out_memory=pltpu.VMEM, limit=None):
    args = [
        pltpu.with_memory_space_constraint(a, pltpu.VMEM) if spec is VMEM else a
        for a, spec in zip(args, in_specs)
    ]
    if isinstance(out_shape, list):
        shapes = [pltpu.VMEM(*o) for o in out_shape]
    else:
        shapes = out_memory(*out_shape) if out_memory else jax.ShapeDtypeStruct(*out_shape)
    return pl.pallas_call(
        kernel,
        out_shape=shapes,
        in_specs=in_specs,
        out_specs=[VMEM] * len(out_shape) if isinstance(out_shape, list) else VMEM,
        scratch_shapes=list(scratch),
        compiler_params=pltpu.CompilerParams(vmem_limit_bytes=limit),
    )(*args)


def split(v):
    high = v.astype(BF16)
    return high, (v - high.astype(F32)).astype(BF16)


def iota(shape, axis):
    return lax.broadcasted_iota(jnp.int32, shape, axis)


def select_kernel(index_ref, hidden_ref, out_ref):
    chosen = jnp.where(iota((256, 64), 0) == index_ref[...], 1.0, 0.0).astype(BF16)
    out_ref[...] = lax.dot_general(
        chosen, hidden_ref[...], (((0,), (0,)), ((), ())), preferred_element_type=F32
    ).astype(BF16)


def live_kernel(count_ref, out_ref):
    out_ref[...] = jnp.broadcast_to(count_ref[...], (8, 128))


def hold_kernel(head_ref, out_ref, sem):
    copy = pltpu.make_async_copy(head_ref, out_ref, sem)
    copy.start()
    copy.wait()


def logits_kernel(core_ref, own_ref, other_ref, head_ref, out_ref):
    first = core_ref[0] == 0
    lhs = []
    for group in range(2):
        rows = pl.ds(group * 256, 256)
        features = []
        for x in range(4):
            picks = [16 * (1 - group) + 4 * o + x for o in range(4)]
            own = jnp.concatenate([own_ref[p] for p in picks], axis=0)
            other = jnp.concatenate([other_ref[p] for p in picks], axis=0)
            features.append(jnp.where(first, own, other))
            features.append(jnp.where(first, other, own))
        lhs.append(jnp.concatenate(features, axis=1))
    for n in range(6):
        for group in range(2):
            part = jnp.dot(lhs[group], head_ref[:, n * 256 : n * 256 + 256], preferred_element_type=F32).astype(BF16)
            for owner in range(4):
                out_ref[group * 4 + owner, :, pl.ds(n * 256, 256)] = part[owner * 64 : owner * 64 + 64]


def project_kernel(core_ref, parts_ref, basis_ref, keep_ref, send_ref, held_ref, tiles_ref, sems):
    copies = [
        pltpu.make_async_copy(basis_ref.at[pl.ds(2 * j, 2)], held_ref.at[j], sems.at[j]) for j in range(4)
    ]
    for copy in copies:
        copy.start()
    logits = parts_ref[0].astype(F32)
    for i in range(1, 8):
        logits = logits + parts_ref[i].astype(F32)
    top_high, top_low = split(jnp.max(logits, axis=1, keepdims=True))
    top_high, top_low = top_high.astype(F32), top_low.astype(F32)
    weights = jnp.exp(logits - (top_high + top_low))
    den_high, den_low = split(jnp.sum(weights, axis=1, keepdims=True))
    wei_high, wei_low = split(jnp.sum(weights * logits, axis=1, keepdims=True))
    lane = iota((64, 128), 1)
    stats = jnp.zeros((64, 128), F32)
    for i, v in enumerate([top_high, top_low, den_high, den_low, wei_high, wei_low]):
        stats = jnp.where(lane == i, v.astype(F32), stats)
    stats = jnp.concatenate([jnp.zeros((64, 128), F32), stats], axis=0).T[0:16, :]
    high, low = split(logits)
    lhs = jnp.concatenate([high, low, jnp.ones((16, 1536), BF16)], axis=0)
    row, lane = iota((16, 128), 0), iota((16, 128), 1)
    for j in range(4):
        copies[j].wait()
        rhs = jnp.concatenate([held_ref[j, 0], held_ref[j, 1]], axis=1)
        both = jnp.dot(lhs, rhs, preferred_element_type=F32)
        turned = jnp.concatenate([both[0:64] + both[64:128], jnp.zeros((64, 256), F32)], axis=0).T
        for half in range(2):
            sums_high, sums_low = split(both[128:136, half * 128 : half * 128 + 128])
            sums_high, sums_low = sums_high.astype(F32), sums_low.astype(F32)
            for block in range(8):
                start = half * 128 + block * 16
                shift = (64 - 16 * block) % 128
                line_high = pltpu.roll(sums_high, shift, 1)[0:1]
                line_low = pltpu.roll(sums_low, shift, 1)[0:1]
                extra = jnp.where(row == 6, line_high, jnp.where(row == 7, line_low, stats))
                tile = jnp.where(lane < 64, turned[start : start + 16], extra)
                tiles_ref[block % 2, 8 * j + 4 * half + block // 2] = tile.astype(BF16)
    keep_ref[...] = tiles_ref[core_ref[0]]
    send_ref[...] = tiles_ref[1 - core_ref[0]]


def merge(tiles):
    tops = [t[0:1] + t[1:2] for t in tiles]
    top = tops[0]
    for t in tops[1:]:
        top = jnp.maximum(top, t)
    denominator, weighted, sums = 0.0, 0.0, 0.0
    for mine, tile in zip(tops, tiles):
        scale = jnp.exp(mine - top)
        denominator = denominator + scale * (tile[2:3] + tile[3:4])
        weighted = weighted + scale * (tile[4:5] + tile[5:6])
        sums = sums + (tile[6:7] + tile[7:8])
    return top, denominator, weighted, sums


def pair_kernel(keep_ref, recv_ref, out_ref):
    top, denominator, weighted, _ = merge([keep_ref[0].astype(F32), recv_ref[0].astype(F32)])
    row, lane = iota((16, 128), 0), iota((16, 128), 1)
    stats = jnp.zeros((16, 128), F32)
    for i, v in enumerate([h for v in (top, denominator, weighted) for h in split(v)]):
        stats = jnp.where(row == i, v.astype(F32), stats)
    shared = jnp.logical_and(lane >= 64, row < 6)
    for i in range(32):
        keep, recv = keep_ref[i].astype(F32), recv_ref[i].astype(F32)
        sums_high, sums_low = split((keep[6:7] + keep[7:8]) + (recv[6:7] + recv[7:8]))
        tile = jnp.where(row == 6, sums_high.astype(F32), sums_low.astype(F32))
        tile = jnp.where(jnp.logical_and(lane >= 64, row < 8), tile, keep + recv)
        out_ref[i] = jnp.where(shared, stats, tile).astype(BF16)


def finish_kernel(count_ref, in_ref, out_ref):
    tiles = [in_ref[i].astype(F32) for i in range(32)]
    total = tiles[0]
    for t in tiles[1:]:
        total = total + t
    _, denominator, weighted, sums = merge(tiles)
    expected = pltpu.roll(jnp.broadcast_to(weighted / denominator, (8, 128)), 64, 1)[0:1]
    row, lane = iota((16, 128), 0), iota((16, 128), 1)
    column = jnp.sum(jnp.where(lane == row + 64, sums, 0.0), axis=1, keepdims=True)
    result = jnp.where(lane < count_ref[0:1, :], total - expected * column, 0.0)
    out_ref[...] = result[:, 0:64]


def shards(hidden, head_weight, vocab_basis, keep_index, counts):
    def exchange(v, axes):
        return lax.all_to_all(v, axes, 0, 0, tiled=True)

    core = lax.axis_index("c").astype(jnp.int32).reshape(1)
    owned = call(select_kernel, ((64, 128), BF16), [OUTER, OUTER], keep_index.reshape(1, 64), hidden)
    late_counts, owned = lax.optimization_barrier((counts, owned))
    basis = lax.all_gather(vocab_basis, "z")
    pairs = [((z * 8 + y) * 8 + k, (y * 8 + (z + 4) % 8) * 8 + k) for z in range(8) for y in range(8) for k in range(8)]
    moved = lax.ppermute(owned, ("z", "y", "x", "c"), pairs)
    live = call(live_kernel, ((8, 128), jnp.int32), [OUTER], late_counts.reshape(1, 1))
    mine = exchange(jnp.broadcast_to(moved[None], (32, 64, 128)), ("y", "x"))
    theirs = lax.ppermute(mine, "c", [(0, 1), (1, 0)])
    held = call(
        hold_kernel,
        ((1024, 1536), BF16),
        [STAY],
        head_weight,
        scratch=[pltpu.SemaphoreType.DMA],
        limit=58 << 20,
    )
    parts = call(
        logits_kernel,
        ((8, 64, 1536), BF16),
        [SMEM, VMEM, VMEM, VMEM],
        core,
        mine,
        theirs,
        held,
        limit=32 << 20,
    )
    keep, send = call(
        project_kernel,
        [((32, 16, 128), BF16), ((32, 16, 128), BF16)],
        [SMEM, VMEM, STAY],
        core,
        exchange(parts, "z"),
        basis,
        scratch=[
            pltpu.VMEM((4, 2, 1536, 128), BF16),
            pltpu.VMEM((2, 32, 16, 128), BF16),
            pltpu.SemaphoreType.DMA((4,)),
        ],
    )
    tiles = call(pair_kernel, ((32, 16, 128), BF16), [VMEM, VMEM], keep, lax.ppermute(send, "c", [(0, 1), (1, 0)]))
    tiles = exchange(tiles, ("y", "x"))
    return call(finish_kernel, ((16, 64), F32), [VMEM, VMEM], live, tiles, out_memory=None).T


def solution(mesh):
    grid = Mesh(mesh.devices.reshape(8, 8, 4, 2), ALL)
    rows, cols = "z", ("y", "x", "c")
    in_specs = (P(rows, cols), P(rows, cols), P(cols, rows), P(rows), P(rows))
    return jax.shard_map(shards, mesh=grid, in_specs=in_specs, out_specs=P(rows, cols), check_vma=False)
```

```python
import jax
import jax.numpy as jnp
from jax import lax
from jax.experimental import pallas as pl
from jax.experimental.pallas import tpu as pltpu
from jax.sharding import Mesh, PartitionSpec as P


F32 = jnp.float32
BF16 = jnp.bfloat16
ALL = ("z", "y", "x", "c")
VMEM = pl.BlockSpec(memory_space=pltpu.VMEM)
SMEM = pl.BlockSpec(memory_space=pltpu.SMEM)
OUTER = pl.BlockSpec(memory_space=pltpu.VMEM)
STAY = pl.BlockSpec(memory_space=pl.ANY)


def call(kernel, out_shape, in_specs, *args, scratch=(), out_memory=pltpu.VMEM, limit=None):
    args = [
        pltpu.with_memory_space_constraint(a, pltpu.VMEM) if spec is VMEM else a
        for a, spec in zip(args, in_specs)
    ]
    if isinstance(out_shape, list):
        shapes = [pltpu.VMEM(*o) for o in out_shape]
    else:
        shapes = out_memory(*out_shape) if out_memory else jax.ShapeDtypeStruct(*out_shape)
    return pl.pallas_call(
        kernel,
        out_shape=shapes,
        in_specs=in_specs,
        out_specs=[VMEM] * len(out_shape) if isinstance(out_shape, list) else VMEM,
        scratch_shapes=list(scratch),
        compiler_params=pltpu.CompilerParams(vmem_limit_bytes=limit),
    )(*args)


def split(v):
    high = v.astype(BF16)
    return high, (v - high.astype(F32)).astype(BF16)


def iota(shape, axis):
    return lax.broadcasted_iota(jnp.int32, shape, axis)


def select_kernel(index_ref, hidden_ref, count_ref, out_ref, live_ref):
    live_ref[...] = jnp.broadcast_to(count_ref[...], (8, 128))
    chosen = jnp.where(iota((256, 64), 0) == index_ref[...], 1.0, 0.0).astype(BF16)
    out_ref[...] = lax.dot_general(
        chosen, hidden_ref[...], (((0,), (0,)), ((), ())), preferred_element_type=F32
    ).astype(BF16)


def hold_kernel(head_ref, out_ref, sem):
    copy = pltpu.make_async_copy(head_ref, out_ref, sem)
    copy.start()
    copy.wait()


def logits_kernel(core_ref, own_ref, other_ref, head_ref, out_ref):
    first = core_ref[0] == 0
    lhs = []
    for group in range(2):
        rows = pl.ds(group * 256, 256)
        features = []
        for x in range(4):
            picks = [16 * (1 - group) + 4 * o + x for o in range(4)]
            own = jnp.concatenate([own_ref[p] for p in picks], axis=0)
            other = jnp.concatenate([other_ref[p] for p in picks], axis=0)
            features.append(jnp.where(first, own, other))
            features.append(jnp.where(first, other, own))
        lhs.append(jnp.concatenate(features, axis=1))
    for n in range(6):
        for group in range(2):
            part = jnp.dot(lhs[group], head_ref[:, n * 256 : n * 256 + 256], preferred_element_type=F32).astype(BF16)
            for owner in range(4):
                out_ref[group * 4 + owner, :, pl.ds(n * 256, 256)] = part[owner * 64 : owner * 64 + 64]


def project_kernel(core_ref, parts_ref, basis_ref, keep_ref, send_ref, held_ref, tiles_ref, sems):
    copies = [
        pltpu.make_async_copy(basis_ref.at[pl.ds(2 * j, 2)], held_ref.at[j], sems.at[j]) for j in range(4)
    ]
    for copy in copies:
        copy.start()
    logits = parts_ref[0].astype(F32)
    for i in range(1, 8):
        logits = logits + parts_ref[i].astype(F32)
    top_high, top_low = split(jnp.max(logits, axis=1, keepdims=True))
    top_high, top_low = top_high.astype(F32), top_low.astype(F32)
    weights = jnp.exp(logits - (top_high + top_low))
    den_high, den_low = split(jnp.sum(weights, axis=1, keepdims=True))
    wei_high, wei_low = split(jnp.sum(weights * logits, axis=1, keepdims=True))
    lane = iota((64, 128), 1)
    stats = jnp.zeros((64, 128), F32)
    for i, v in enumerate([top_high, top_low, den_high, den_low, wei_high, wei_low]):
        stats = jnp.where(lane == i, v.astype(F32), stats)
    stats = jnp.concatenate([jnp.zeros((64, 128), F32), stats], axis=0).T[0:16, :]
    high, low = split(logits)
    lhs = jnp.concatenate([high, low, jnp.ones((16, 1536), BF16)], axis=0)
    row, lane = iota((16, 128), 0), iota((16, 128), 1)
    for j in range(4):
        copies[j].wait()
        rhs = jnp.concatenate([held_ref[j, 0], held_ref[j, 1]], axis=1)
        both = jnp.dot(lhs, rhs, preferred_element_type=F32)
        turned = jnp.concatenate([both[0:64] + both[64:128], jnp.zeros((64, 256), F32)], axis=0).T
        for half in range(2):
            sums_high, sums_low = split(both[128:136, half * 128 : half * 128 + 128])
            sums_high, sums_low = sums_high.astype(F32), sums_low.astype(F32)
            for block in range(8):
                start = half * 128 + block * 16
                shift = (64 - 16 * block) % 128
                line_high = pltpu.roll(sums_high, shift, 1)[0:1]
                line_low = pltpu.roll(sums_low, shift, 1)[0:1]
                extra = jnp.where(row == 6, line_high, jnp.where(row == 7, line_low, stats))
                tile = jnp.where(lane < 64, turned[start : start + 16], extra)
                tiles_ref[block % 2, 8 * j + 4 * half + block // 2] = tile.astype(BF16)
    keep_ref[...] = tiles_ref[core_ref[0]]
    send_ref[...] = tiles_ref[1 - core_ref[0]]


def merge(tiles):
    tops = [t[0:1] + t[1:2] for t in tiles]
    top = tops[0]
    for t in tops[1:]:
        top = jnp.maximum(top, t)
    denominator, weighted, sums = 0.0, 0.0, 0.0
    for mine, tile in zip(tops, tiles):
        scale = jnp.exp(mine - top)
        denominator = denominator + scale * (tile[2:3] + tile[3:4])
        weighted = weighted + scale * (tile[4:5] + tile[5:6])
        sums = sums + (tile[6:7] + tile[7:8])
    return top, denominator, weighted, sums


def pair_kernel(keep_ref, recv_ref, out_ref):
    top, denominator, weighted, _ = merge([keep_ref[0].astype(F32), recv_ref[0].astype(F32)])
    row, lane = iota((16, 128), 0), iota((16, 128), 1)
    stats = jnp.zeros((16, 128), F32)
    for i, v in enumerate([h for v in (top, denominator, weighted) for h in split(v)]):
        stats = jnp.where(row == i, v.astype(F32), stats)
    shared = jnp.logical_and(lane >= 64, row < 6)
    for i in range(32):
        keep, recv = keep_ref[i].astype(F32), recv_ref[i].astype(F32)
        sums_high, sums_low = split((keep[6:7] + keep[7:8]) + (recv[6:7] + recv[7:8]))
        tile = jnp.where(row == 6, sums_high.astype(F32), sums_low.astype(F32))
        tile = jnp.where(jnp.logical_and(lane >= 64, row < 8), tile, keep + recv)
        out_ref[i] = jnp.where(shared, stats, tile).astype(BF16)


def finish_kernel(count_ref, in_ref, out_ref):
    tiles = [in_ref[i].astype(F32) for i in range(32)]
    total = tiles[0]
    for t in tiles[1:]:
        total = total + t
    _, denominator, weighted, sums = merge(tiles)
    expected = pltpu.roll(jnp.broadcast_to(weighted / denominator, (8, 128)), 64, 1)[0:1]
    row, lane = iota((16, 128), 0), iota((16, 128), 1)
    column = jnp.sum(jnp.where(lane == row + 64, sums, 0.0), axis=1, keepdims=True)
    result = jnp.where(lane < count_ref[0:1, :], total - expected * column, 0.0)
    out_ref[...] = result[:, 0:64]


def shards(hidden, head_weight, vocab_basis, keep_index, counts):
    def exchange(v, axes):
        return lax.all_to_all(v, axes, 0, 0, tiled=True)

    core = lax.axis_index("c").astype(jnp.int32).reshape(1)
    owned, live = call(
        select_kernel,
        [((64, 128), BF16), ((8, 128), jnp.int32)],
        [OUTER, OUTER, OUTER],
        keep_index.reshape(1, 64),
        hidden,
        counts.reshape(1, 1),
    )
    late_basis, owned = lax.optimization_barrier((vocab_basis, owned))
    basis = lax.all_gather(late_basis, "z")
    pairs = [((z * 8 + y) * 8 + k, (y * 8 + (z + 4) % 8) * 8 + k) for z in range(8) for y in range(8) for k in range(8)]
    moved = lax.ppermute(owned, ("z", "y", "x", "c"), pairs)
    mine = exchange(jnp.broadcast_to(moved[None], (32, 64, 128)), ("y", "x"))
    theirs = lax.ppermute(mine, "c", [(0, 1), (1, 0)])
    held = call(
        hold_kernel,
        ((1024, 1536), BF16),
        [STAY],
        head_weight,
        scratch=[pltpu.SemaphoreType.DMA],
        limit=58 << 20,
    )
    parts = call(
        logits_kernel,
        ((8, 64, 1536), BF16),
        [SMEM, VMEM, VMEM, VMEM],
        core,
        mine,
        theirs,
        held,
        limit=32 << 20,
    )
    keep, send = call(
        project_kernel,
        [((32, 16, 128), BF16), ((32, 16, 128), BF16)],
        [SMEM, VMEM, STAY],
        core,
        exchange(parts, "z"),
        basis,
        scratch=[
            pltpu.VMEM((4, 2, 1536, 128), BF16),
            pltpu.VMEM((2, 32, 16, 128), BF16),
            pltpu.SemaphoreType.DMA((4,)),
        ],
    )
    tiles = call(pair_kernel, ((32, 16, 128), BF16), [VMEM, VMEM], keep, lax.ppermute(send, "c", [(0, 1), (1, 0)]))
    tiles = exchange(tiles, ("y", "x"))
    return call(finish_kernel, ((16, 64), F32), [VMEM, VMEM], live, tiles, out_memory=None).T


def solution(mesh):
    grid = Mesh(mesh.devices.reshape(8, 8, 4, 2), ALL)
    rows, cols = "z", ("y", "x", "c")
    in_specs = (P(rows, cols), P(rows, cols), P(cols, rows), P(rows), P(rows))
    return jax.shard_map(shards, mesh=grid, in_specs=in_specs, out_specs=P(rows, cols), check_vma=False)
```
